32 devices in a mesh: grp: 4 (over x, core), sub: 8 (over z, y).
Axes of the slice: x: 2, y: 2, z: 4, core: 2. Of those that a mesh axis runs over, the one named last changes fastest.
Arguments:
- points: bfloat16 [32768, 1024], P(('grp', 'sub')), may hold values from -16 to 16
- level1_ids: int32 [32768], P(('grp', 'sub')), may hold values from 0 to 255
- level2_ids: int32 [32768], P(('grp', 'sub')), may hold values from 0 to 8191, as said below
- level3_ids: int32 [32768], P(('grp', 'sub')), may hold values from 0 to 255
- needed: int32 [32, 32], P(('grp', 'sub')), may hold values from 0 to 8191, as said below
- centroids1: bfloat16 [65536, 1024], P(('grp', 'sub')), may hold values from -6 to 6
- centroids2: bfloat16 [4, 8192, 1024], P('grp', 'sub'), may hold values from -3 to 3
- centroids3: bfloat16 [256, 1024], replicated, may hold values from -6 to 6
Outputs:
- level1_new: float32 [65536, 1024], P(('grp', 'sub'))
- level2_new: float32 [4, 8192, 1024], P('grp', 'sub')
- level3_new: float32 [256, 1024], replicated
The draws below stay inside these ranges and needn't reach their ends.
Inputs may be any that keep to these rules, and one draw needn't show every extreme that they name: `needed`: each row lists distinct blocks; a row names at most 2 blocks held by one device (blocks of device o are o * 256 to o * 256 + 255), and names exactly 2 of some device's blocks. `level2_ids`: of one device's points, at most 256 have level-2 ids in any one range r * 8192 // 8 to (r + 1) * 8192 // 8 - 1, and exactly 256 in some range.
All inputs are finite; a program needn't handle non-finite values.
Results may differ from the reference program's by a relative error of at most 0.0055.
Values may be sent and summed in bfloat16 or wider, within the bound.
A program may use at most 128 MiB of HBM per device.

```python
import math
import jax
import jax.numpy as jnp
from jax import lax

D = 1024
BLK = 8
CAP = 2
K2 = 8192
K3 = 256
PTS_DEV = 1024
K1 = 65536
NB_DEV = 256
NEED = 32
CAP2 = 256
POINTS = 32768
N_GRP = 4
N_SUB = 8
DEVICES = 32


def level3_labels(key):
    base = jax.random.fold_in(key, 31)

    def per_device(dev_key, device):
        first_key, second_key, third_key = jax.random.split(dev_key, 3)
        home_cluster = device * K3 // DEVICES
        width_near = max(K3 // DEVICES, 1)
        near_ids = home_cluster + jax.random.randint(first_key, (PTS_DEV,), 0, width_near)
        far_ids = jax.random.randint(second_key, (PTS_DEV,), 0, K3)
        choose_near = jax.random.randint(third_key, (PTS_DEV,), 0, 4) < 3
        return jnp.where(choose_near, near_ids, far_ids)
    keys = jax.random.split(base, DEVICES)
    return jax.vmap(per_device)(keys, jnp.arange(DEVICES)).reshape(-1).astype(jnp.int32)


def needed_lists(key):
    base = jax.random.fold_in(key, 61)

    def per_device(dev_key):
        first_key, second_key, third_key = jax.random.split(dev_key, 3)
        hot_owner = jax.random.randint(first_key, (), 0, DEVICES)
        slot_ids = jnp.arange(DEVICES * CAP)
        random_bits = jax.random.randint(second_key, (DEVICES * CAP,), 0, 1 << 18)
        scores = random_bits * (DEVICES * CAP) + slot_ids + jnp.where(slot_ids // CAP == hot_owner, 1 << 30, 0)
        chosen = lax.top_k(scores, NEED)[1]
        owner_of = chosen // CAP
        offset = jax.random.randint(third_key, (DEVICES,), 0, NB_DEV)
        local_block = (offset[owner_of] + chosen % CAP) % NB_DEV
        return owner_of * NB_DEV + local_block
    return jax.vmap(per_device)(jax.random.split(base, DEVICES)).astype(jnp.int32)


def draw_needed(key, part):
    return needed_lists(key)


def draw_level1_ids(key, part):
    first_key, second_key = jax.random.split(jax.random.fold_in(key, 71))
    picks = jax.random.randint(first_key, (DEVICES, PTS_DEV), 0, NEED)
    within = jax.random.randint(second_key, (DEVICES, PTS_DEV), 0, BLK)
    return (picks * BLK + within).reshape(-1).astype(jnp.int32)


def draw_level2_ids(key, part):
    base = jax.random.fold_in(key, 51)
    group_keys = jax.random.split(jax.random.fold_in(base, 1), DEVICES // N_SUB)
    hot_by_group = jax.vmap(lambda group_key: jax.random.randint(group_key, (), 0, N_SUB))(group_keys)
    shard_rows = K2 // N_SUB

    def per_device(dev_key, hot_owner):
        first_key, second_key, third_key = jax.random.split(dev_key, 3)
        slot_ids = jnp.arange(N_SUB * CAP2)
        slot_owner = slot_ids // CAP2
        random_bits = jax.random.randint(first_key, (N_SUB * CAP2,), 0, 1 << 16)
        scores = random_bits * (N_SUB * CAP2) + slot_ids + jnp.where(slot_owner == hot_owner, 1 << 30, 0)
        chosen = lax.top_k(scores, PTS_DEV)[1]
        chosen = chosen[jax.random.permutation(second_key, PTS_DEV)]
        local_block = jax.random.randint(third_key, (PTS_DEV,), 0, shard_rows)
        return chosen // CAP2 * shard_rows + local_block
    keys = jax.random.split(base, DEVICES)
    hot_each = jnp.repeat(hot_by_group, N_SUB)
    return jax.vmap(per_device)(keys, hot_each).reshape(-1).astype(jnp.int32)


def draw_level3_ids(key, part):
    return level3_labels(key)


def draw_points(key, part):
    labels = level3_labels(key)
    base = jax.random.fold_in(key, 41)
    first_key, second_key, third_key = jax.random.split(base, 3)
    offset_key = jax.random.fold_in(base, 5)
    cluster_means = jnp.clip(jax.random.normal(first_key, (K3, D), jnp.float32), -4.0, 4.0)
    device_shift = jnp.clip(jax.random.normal(offset_key, (DEVICES, D), jnp.float32), -2.0, 2.0)
    device_of = jnp.arange(PTS_DEV * DEVICES) // PTS_DEV
    row_scale = jnp.exp(jax.random.uniform(second_key, (PTS_DEV * DEVICES, 1), jnp.float32, math.log(0.3), math.log(3.0)))
    jitter = jnp.clip(jax.random.normal(third_key, (PTS_DEV * DEVICES, D), jnp.float32), -4.0, 4.0)
    values = cluster_means[labels] + device_shift[device_of] + row_scale * jitter
    return jnp.clip(values, -16.0, 16.0).astype(jnp.bfloat16)


def shard_levels(stream_key, dims, pieces, low, largest):
    def one(position, blocks):
        steps = jax.random.uniform(jax.random.fold_in(jax.random.fold_in(stream_key, 6), position), (blocks,), jnp.float32, low / len(pieces), largest / len(pieces))
        return jnp.repeat(jnp.exp(steps), dims[position] // blocks).reshape((-1,) + (1,) * (len(dims) - position - 1))

    level = one(*pieces[0])
    for cut in pieces[1:]:
        level = level * one(*cut)
    return level


def centred(rng, extent, deviation, bound, shards=(), kind=jnp.bfloat16):
    array = deviation * jax.random.normal(rng, extent, jnp.float32)
    if shards:
        array = array * shard_levels(rng, extent, shards, -0.22, 0.18)
    return jnp.clip(array, -bound, bound).astype(kind)


def setup_inputs(seed: int = 0) -> dict:
    seeds = jax.random.split(jax.random.key(seed), 9)
    return {
        "points": draw_points(jax.random.fold_in(seeds[8], 71), 0),
        "level1_ids": draw_level1_ids(jax.random.fold_in(seeds[8], 71), 0),
        "level2_ids": draw_level2_ids(jax.random.fold_in(seeds[8], 71), 0),
        "level3_ids": draw_level3_ids(jax.random.fold_in(seeds[8], 71), 0),
        "needed": draw_needed(jax.random.fold_in(seeds[8], 71), 0),
        "centroids1": centred(seeds[5], (K1, D), 1.0, 6.0, ((0, 32),)),
        "centroids2": centred(seeds[6], (N_GRP, K2, D), 0.5, 3.0, ((0, 4), (1, 8))),
        "centroids3": centred(seeds[7], (K3, D), 1.0, 6.0),
    }


def rounded(values):
    return lax.optimization_barrier(values.astype(jnp.bfloat16)).astype(jnp.float32)


def reference(points, level1_ids, level2_ids, level3_ids, needed, centroids1, centroids2, centroids3):
    device_of = (jnp.arange(POINTS, dtype=jnp.int32) // PTS_DEV).astype(jnp.int32)
    entry = (level1_ids // BLK).astype(jnp.int32)
    global1 = (needed[device_of, entry] * BLK + level1_ids % BLK).astype(jnp.int32)
    values = points.astype(jnp.float32)
    nearest = centroids1[global1].astype(jnp.float32)
    spread = jnp.sum((values - nearest) ** 2, axis=1) / D
    weight = rounded(1.0 / (1.0 + spread))
    weighted = weight[:, None] * values
    sums1 = jax.ops.segment_sum(weighted, global1, num_segments=K1)
    mass1 = jax.ops.segment_sum(weight, global1, num_segments=K1)
    level1_new = (centroids1.astype(jnp.float32) + sums1) / (1.0 + mass1[:, None])

    group_index = jnp.arange(DEVICES, dtype=jnp.int32) // N_SUB

    def add_device(totals, inputs):
        sums_acc, mass_acc = totals
        row_block, labels, masses, group_at = inputs
        device_sums = rounded(jax.ops.segment_sum(row_block, labels, num_segments=K2))
        device_mass = rounded(jax.ops.segment_sum(masses, labels, num_segments=K2))
        return (sums_acc.at[group_at].add(device_sums), mass_acc.at[group_at].add(device_mass)), None

    start = (jnp.zeros((N_GRP, K2, D), jnp.float32), jnp.zeros((N_GRP, K2), jnp.float32))
    (sums2, mass2), _ = lax.scan(add_device, start, (weighted.reshape(DEVICES, PTS_DEV, D), level2_ids.reshape(DEVICES, PTS_DEV), weight.reshape(DEVICES, PTS_DEV), group_index))
    level2_new = (centroids2.astype(jnp.float32) + sums2) / (1.0 + mass2[:, :, None])

    sums3 = jax.ops.segment_sum(weighted, level3_ids, num_segments=K3)
    mass3 = jax.ops.segment_sum(weight, level3_ids, num_segments=K3)
    level3_new = (centroids3.astype(jnp.float32) + sums3) / (1.0 + mass3[:, None])
    return level1_new, level2_new, level3_new
```

```python
import functools

import jax
import jax.numpy as jnp
from jax import lax
from jax.experimental import pallas as pl
from jax.experimental.pallas import tpu as pltpu
from jax.sharding import PartitionSpec as P

BLK = 8
CAP = 2
LANES = 128
MESH = pl.DeviceIdType.MESH
F32 = jnp.float32
BF16 = jnp.bfloat16


def iota(shape, dim):
    return lax.broadcasted_iota(jnp.int32, shape, dim)


def step_kernel(
    groups,
    subs,
    served,
    points,
    pidx_col,
    pidx_row,
    sidx_row,
    l3_row,
    lrows,
    cent3,
    back_out,
    l2_out,
    meta_out,
    l3_out,
    fetched,
    back_src,
    l2_src,
    meta_src,
    w_row,
    a_src,
    a_dst,
    b_src,
    b_dst,
    c_buf,
    e1s,
    e1r,
    e3s,
    e3r,
    l2s,
    l2r,
    ms,
    mr,
    as_,
    ar,
    bs,
    br,
    cs,
    cr,
    ds_,
    dr,
    lsem,
):
    n = groups * subs
    g_me, s_me = lax.axis_index("grp"), lax.axis_index("sub")
    me = g_me * subs + s_me
    slots = CAP * BLK
    pts, feat = points.shape
    cap = l2_src.shape[1]
    rows_a = a_src.shape[1]
    rows_b = b_src.shape[1]

    def flat(k):
        t = lax.rem(me + k, n)
        return (lax.div(t, subs), lax.rem(t, subs))

    def sub_peer(k):
        return lax.rem(s_me + k, subs)

    def grp_peer(k):
        return lax.rem(g_me + k, groups)

    barrier = pltpu.get_barrier_semaphore()

    @pl.loop(1, n)
    def _(k):
        pl.semaphore_signal(barrier, inc=1, device_id=flat(k), device_id_type=MESH)

    pl.semaphore_wait(barrier, n - 1)

    def remote(src, dst, ss, rs, dev):
        return pltpu.make_async_remote_copy(
            src_ref=src, dst_ref=dst, send_sem=ss, recv_sem=rs, device_id=dev, device_id_type=MESH
        )

    def e1(k):
        t = lax.rem(me + k, n)
        return remote(served.at[t], fetched.at[me], e1s.at[k], e1r.at[k], flat(k))

    def e3(k):
        t = lax.rem(me + k, n)
        return remote(back_src.at[t], back_out.at[me], e3s.at[k], e3r.at[k], flat(k))

    def e2(k):
        t = sub_peer(k)
        return remote(l2_src.at[t], l2_out.at[s_me], l2s.at[k], l2r.at[k], (g_me, t))

    def em(k):
        t = sub_peer(k)
        return remote(meta_src.at[t], meta_out.at[s_me], ms.at[k], mr.at[k], (g_me, t))

    def ea(k):
        t = grp_peer(k)
        return remote(a_src.at[t], a_dst.at[g_me], as_.at[k], ar.at[k], (t, s_me))

    def eb(k):
        t = sub_peer(k)
        return remote(b_src.at[t], b_dst.at[s_me], bs.at[k], br.at[k], (g_me, t))

    def ec(k):
        t = sub_peer(k)
        return remote(c_buf.at[s_me], c_buf.at[s_me], cs.at[k], cr.at[k], (g_me, t))

    def ed(k):
        t = grp_peer(k)
        return remote(c_buf, l3_out.at[g_me], ds_.at[k], dr.at[k], (t, s_me))

    @pl.loop(1, n)
    def _(k):
        e1(k).start()

    fetched[me] = served[me]

    def route(t):
        slot = iota((cap, pts), 0) + t * cap
        return jnp.where(sidx_row[...] == slot, F32(1), F32(0)).astype(BF16)

    def build(k):
        t = sub_peer(k)
        l2_src[t] = jnp.dot(route(t), points[...], preferred_element_type=F32).astype(BF16)

    half = subs // 2

    @pl.loop(1, half)
    def _(k):
        build(k)
        e2(k).start()

    @pl.loop(1, n)
    def _(k):
        e1(k).wait_recv()

    tile = LANES
    total = n * slots

    @pl.loop(0, pts // tile)
    def _(i):
        at = pl.ds(pl.multiple_of(i * tile, tile), tile)
        hot = jnp.where(pidx_col[at, :] == iota((tile, total), 1), F32(1), F32(0)).astype(BF16)
        near = jnp.dot(hot, fetched[...].reshape(total, feat), preferred_element_type=F32)
        diff = points[at, :].astype(F32) - near
        spread = jnp.sum(diff * diff, axis=1, keepdims=True) / feat
        w = (1.0 / (1.0 + spread)).astype(BF16).astype(F32)
        eye = iota((tile, tile), 0) == iota((tile, tile), 1)
        w_row[:, at] = jnp.sum(jnp.where(eye, w, F32(0)), axis=0, keepdims=True)

    per = tile // slots

    def sums(labels, base):
        hot = jnp.where(labels == iota((tile, pts), 0) + base, w_row[...], F32(0))
        mass = jnp.sum(hot, axis=1, keepdims=True)
        return jnp.dot(hot.astype(BF16), points[...], preferred_element_type=F32), mass

    @pl.loop(0, total // tile)
    def _(i):
        s, m = sums(pidx_row[...], i * tile)
        at = pl.ds(i * per, per)
        back_src[at, :, :feat] = s.astype(BF16).reshape(per, slots, feat)
        back_src[at, :, feat:] = (
            jnp.broadcast_to(m, (tile, LANES)).astype(BF16).reshape(per, slots, LANES)
        )

    @pl.loop(1, n)
    def _(k):
        e3(k).start()

    own_back = pltpu.make_async_copy(back_src.at[me], back_out.at[me], lsem.at[0])
    own_back.start()

    k3 = groups * rows_a
    tile3 = min(tile, rows_a)
    for j in range(k3 // tile3):
        hot = jnp.where(l3_row[...] == iota((tile3, pts), 0) + j * tile3, w_row[...], F32(0))
        m = jnp.sum(hot, axis=1, keepdims=True)
        s = jnp.dot(hot.astype(BF16), points[...], preferred_element_type=F32)
        g, r = (j * tile3) // rows_a, (j * tile3) % rows_a
        a_src[g, r : r + tile3, :feat] = s.astype(BF16)
        a_src[g, r : r + tile3, feat:] = jnp.broadcast_to(m, (tile3, LANES)).astype(BF16)
    for k in range(1, groups):
        ea(k).start()

    meta_rows = jnp.where(iota((8, pts), 0) == 0, w_row[...], lrows[...]).astype(BF16)

    def meta(k):
        t = sub_peer(k)
        meta_src[t] = lax.dot_general(
            meta_rows, route(t), (((1,), (1,)), ((), ())), preferred_element_type=F32
        )

    @pl.loop(half, subs)
    def _(k):
        build(k)
        e2(k).start()

    build(0)
    own_l2 = pltpu.make_async_copy(l2_src.at[s_me], l2_out.at[s_me], lsem.at[1])
    own_l2.start()

    for k in range(1, groups):
        ea(k).wait_recv()
    a_dst[g_me] = a_src[g_me]
    acc = a_dst[0].astype(F32)
    for j in range(1, groups):
        acc = acc + a_dst[j].astype(F32)
    for j in range(subs):
        b_src[j] = acc[j * rows_b : (j + 1) * rows_b, :]
    for k in range(1, subs):
        eb(k).start()

    @pl.loop(1, subs)
    def _(k):
        meta(k)
        em(k).start()

    meta(0)
    own_meta = pltpu.make_async_copy(meta_src.at[s_me], meta_out.at[s_me], lsem.at[2])
    own_meta.start()

    for k in range(1, subs):
        eb(k).wait_recv()
    b_dst[s_me] = b_src[s_me]
    acc = b_dst[0]
    for j in range(1, subs):
        acc = acc + b_dst[j]
    c_buf[s_me] = (cent3[g_me, s_me] + acc[:, :feat]) / (1.0 + acc[:, feat : feat + 1])
    for k in range(1, subs):
        ec(k).start()
    for k in range(1, subs):
        ec(k).wait_recv()
    for k in range(1, groups):
        ed(k).start()
    own_l3 = pltpu.make_async_copy(c_buf, l3_out.at[g_me], lsem.at[3])
    own_l3.start()

    own_back.wait()
    own_l2.wait()
    own_meta.wait()
    own_l3.wait()
    for k in range(1, groups):
        ed(k).wait_recv()

    @pl.loop(1, n)
    def _(k):
        e3(k).wait_recv()
        e3(k).wait_send()
        e1(k).wait_send()

    @pl.loop(1, subs)
    def _(k):
        e2(k).wait_recv()
        em(k).wait_recv()
        e2(k).wait_send()
        em(k).wait_send()
        eb(k).wait_send()
        ec(k).wait_send()

    for k in range(1, groups):
        ea(k).wait_send()
        ed(k).wait_send()


def level1_kernel(rows, target, back, cent, out):
    feat = cent.shape[1]
    base = pl.program_id(0) * rows
    hot = jnp.where(
        target[...] == iota((rows, target.shape[1]), 0) + base, F32(1), F32(0)
    ).astype(BF16)
    got = jnp.dot(hot, back[...], preferred_element_type=F32)
    out[...] = (cent[...].astype(F32) + got[:, :feat]) / (1.0 + got[:, feat : feat + 1])


def level2_kernel(rows, labels, weights, got, cent, out):
    base = pl.program_id(0) * rows
    hot = jnp.where(
        labels[...] == iota((rows, labels.shape[1]), 0) + base, weights[...], F32(0)
    )
    mass = jnp.sum(hot, axis=1, keepdims=True)
    sums = jnp.dot(hot.astype(BF16), got[...], preferred_element_type=F32)
    out[...] = (cent[...].astype(F32) + sums) / (1.0 + mass)


def ranks(hits):
    return jnp.sum(jnp.cumsum(hits, axis=0) * hits, axis=1) - 1


def shards(points, level1_ids, level2_ids, level3_ids, needed, centroids1, centroids2, centroids3, *, k2):
    groups, subs = lax.axis_size("grp"), lax.axis_size("sub")
    n = groups * subs
    pts, feat = points.shape
    k1_dev = centroids1.shape[0]
    k3 = centroids3.shape[0]
    blocks_dev = k1_dev // BLK
    slots = CAP * BLK
    need = needed.shape[1]
    wide = feat + LANES

    wanted = needed[0]
    owners = wanted // blocks_dev
    same = owners[:, None] == owners[None, :]
    before = jnp.arange(need)[None, :] < jnp.arange(need)[:, None]
    places = jnp.sum((same & before).astype(jnp.int32), axis=1)
    slot_index = owners * CAP + places
    requests = jnp.sum(
        jnp.where(
            slot_index[None, :] == jnp.arange(n * CAP)[:, None], (wanted % blocks_dev)[None, :], 0
        ),
        axis=1,
    )
    asked = lax.all_to_all(
        requests.reshape(n, CAP), ("grp", "sub"), split_axis=0, concat_axis=0, tiled=True
    )
    target = (asked.reshape(n * CAP, 1) * BLK + jnp.arange(BLK)[None, :]).reshape(n * slots)
    served = centroids1[target].reshape(n, slots, feat)

    entry = level1_ids // BLK
    point_slots = jnp.sum(
        jnp.where(entry[:, None] == jnp.arange(need)[None, :], slot_index[None, :], 0), axis=1
    )
    row_index = point_slots * BLK + level1_ids % BLK

    shard_rows = k2 // subs
    cap = 2 * pts // subs
    range_of = level2_ids // shard_rows
    hits = (range_of[:, None] == jnp.arange(subs)[None, :]).astype(jnp.int32)
    send_index = range_of * cap + ranks(hits)
    local = level2_ids % shard_rows
    lrows = (
        jnp.zeros((8, pts), F32)
        .at[1].set((local // 64).astype(F32))
        .at[2].set((local % 64).astype(F32))
    )

    rows_a = k3 // groups
    rows_b = rows_a // subs
    cent3 = centroids3.astype(F32).reshape(groups, subs, rows_b, feat)
    vmem = pl.BlockSpec(memory_space=pltpu.VMEM)
    anywhere = pl.BlockSpec(memory_space=pl.ANY)
    dma = pltpu.SemaphoreType.DMA
    back, routed, meta, l3 = pl.pallas_call(
        functools.partial(step_kernel, groups, subs),
        out_shape=(
            jax.ShapeDtypeStruct((n, slots, wide), BF16),
            jax.ShapeDtypeStruct((subs, cap, feat), BF16),
            jax.ShapeDtypeStruct((subs, 8, cap), F32),
            jax.ShapeDtypeStruct((groups, subs, rows_b, feat), F32),
        ),
        in_specs=[vmem] * 8,
        out_specs=[anywhere] * 4,
        scratch_shapes=[
            pltpu.VMEM((n, slots, feat), BF16),
            pltpu.VMEM((n, slots, wide), BF16),
            pltpu.VMEM((subs, cap, feat), BF16),
            pltpu.VMEM((subs, 8, cap), F32),
            pltpu.VMEM((1, pts), F32),
            pltpu.VMEM((groups, rows_a, wide), BF16),
            pltpu.VMEM((groups, rows_a, wide), BF16),
            pltpu.VMEM((subs, rows_b, wide), F32),
            pltpu.VMEM((subs, rows_b, wide), F32),
            pltpu.VMEM((subs, rows_b, feat), F32),
            dma((n,)), dma((n,)), dma((n,)), dma((n,)),
            dma((subs,)), dma((subs,)), dma((subs,)), dma((subs,)),
            dma((groups,)), dma((groups,)),
            dma((subs,)), dma((subs,)), dma((subs,)), dma((subs,)),
            dma((groups,)), dma((groups,)),
            dma((4,)),
        ],
        compiler_params=pltpu.CompilerParams(
            collective_id=0, has_side_effects=True, vmem_limit_bytes=56 * 1024 * 1024
        ),
        name="step",
    )(
        served,
        points,
        row_index[:, None],
        row_index[None, :],
        send_index[None, :],
        level3_ids[None, :],
        lrows,
        cent3,
    )

    def tiled(rows, cols):
        return pl.BlockSpec((rows, cols), lambda i: (i, 0))

    def whole(rows, cols):
        return pl.BlockSpec((rows, cols), lambda i: (0, 0))

    tile1 = min(256, k1_dev)
    level1_new = pl.pallas_call(
        functools.partial(level1_kernel, tile1),
        grid=(k1_dev // tile1,),
        in_specs=[whole(1, n * slots), whole(n * slots, wide), tiled(tile1, feat)],
        out_specs=tiled(tile1, feat),
        out_shape=jax.ShapeDtypeStruct((k1_dev, feat), F32),
        name="level1",
    )(target[None, :], back.reshape(n * slots, wide), centroids1)

    labels = (meta[:, 1, :] * 64.0 + meta[:, 2, :]).astype(jnp.int32).reshape(1, subs * cap)
    weights = meta[:, 0, :].reshape(1, subs * cap)
    tile2 = min(256, shard_rows)
    level2_new = pl.pallas_call(
        functools.partial(level2_kernel, tile2),
        grid=(shard_rows // tile2,),
        in_specs=[
            whole(1, subs * cap),
            whole(1, subs * cap),
            whole(subs * cap, feat),
            tiled(tile2, feat),
        ],
        out_specs=tiled(tile2, feat),
        out_shape=jax.ShapeDtypeStruct((shard_rows, feat), F32),
        name="level2",
    )(labels, weights, routed.reshape(subs * cap, feat), centroids2[0])
    return level1_new, level2_new[None], l3.reshape(k3, feat)


def solution(mesh):
    placed = (
        P(("grp", "sub"), None),
        P(("grp", "sub")),
        P(("grp", "sub")),
        P(("grp", "sub")),
        P(("grp", "sub"), None),
        P(("grp", "sub"), None),
        P("grp", "sub", None),
        P(),
    )

    def run(*args):
        return jax.shard_map(
            functools.partial(shards, k2=args[6].shape[1]),
            mesh=mesh,
            in_specs=placed,
            out_specs=(P(("grp", "sub"), None), P("grp", "sub", None), P()),
            check_vma=False,
        )(*args)

    return run
```

```python
import functools

import jax
import jax.numpy as jnp
from jax import lax
from jax.experimental import pallas as pl
from jax.experimental.pallas import tpu as pltpu
from jax.sharding import PartitionSpec as P

BLK = 8
CAP = 2
LANES = 128
MESH = pl.DeviceIdType.MESH
F32 = jnp.float32
BF16 = jnp.bfloat16


def iota(shape, dim):
    return lax.broadcasted_iota(jnp.int32, shape, dim)


def step_kernel(
    groups, subs,
    asked_src, points, pidx_col, pidx_row, sidx_row, l3_row, lrows, cent1, cent2, cent3,
    l1_out, l2_new, l3_out,
    asked, served, fetched, back_src, back_dst, l1_buf,
    l2_src, l2_dst, acc2, mass2, meta_src, meta_dst, w_row,
    a_src, a_dst, b_src, b_dst, c_buf,
    e0s, e0r, e1s, e1r, e3s, e3r, l2s, l2r, ms, mr,
    as_, ar, bs, br, cs, cr, ds_, dr, l1sem, l2sem, lsem,
):
    n = groups * subs
    g_me, s_me = lax.axis_index("grp"), lax.axis_index("sub")
    me = g_me * subs + s_me
    slots = CAP * BLK
    pts, feat = points.shape
    cap = l2_src.shape[1]
    rows_a = a_src.shape[1]
    rows_b = b_src.shape[1]

    def flat(k):
        t = lax.rem(me + k, n)
        return (lax.div(t, subs), lax.rem(t, subs))

    def sub_peer(k):
        return lax.rem(s_me + k, subs)

    def grp_peer(k):
        return lax.rem(g_me + k, groups)

    barrier = pltpu.get_barrier_semaphore()

    @pl.loop(1, n)
    def _(k):
        pl.semaphore_signal(barrier, inc=1, device_id=flat(k), device_id_type=MESH)

    pl.semaphore_wait(barrier, n - 1)

    def remote(src, dst, ss, rs, dev):
        return pltpu.make_async_remote_copy(
            src_ref=src, dst_ref=dst, send_sem=ss, recv_sem=rs, device_id=dev, device_id_type=MESH
        )

    def e0(k):
        t = lax.rem(me + k, n)
        return remote(asked_src.at[t], asked.at[me], e0s.at[k], e0r.at[k], flat(k))

    def e1(k):
        t = lax.rem(me + k, n)
        return remote(served.at[t], fetched.at[me], e1s.at[k], e1r.at[k], flat(k))

    def e3(k):
        t = lax.rem(me + k, n)
        return remote(back_src.at[t], back_dst.at[me], e3s.at[k], e3r.at[k], flat(k))

    def e2(k):
        t = sub_peer(k)
        return remote(l2_src.at[t], l2_dst.at[s_me], l2s.at[k], l2r.at[k], (g_me, t))

    def em(k):
        t = sub_peer(k)
        return remote(meta_src.at[t], meta_dst.at[s_me], ms.at[k], mr.at[k], (g_me, t))

    def ea(k):
        t = grp_peer(k)
        return remote(a_src.at[t], a_dst.at[g_me], as_.at[k], ar.at[k], (t, s_me))

    def eb(k):
        t = sub_peer(k)
        return remote(b_src.at[t], b_dst.at[s_me], bs.at[k], br.at[k], (g_me, t))

    def ec(k):
        t = sub_peer(k)
        return remote(c_buf.at[s_me], c_buf.at[s_me], cs.at[k], cr.at[k], (g_me, t))

    def ed(k):
        t = grp_peer(k)
        return remote(c_buf, l3_out.at[g_me], ds_.at[k], dr.at[k], (t, s_me))

    @pl.loop(1, n)
    def _(k):
        e0(k).start()

    asked[me] = asked_src[me]

    def route(t):
        slot = iota((cap, pts), 0) + t * cap
        return jnp.where(sidx_row[...] == slot, F32(1), F32(0)).astype(BF16)

    def build(k):
        t = sub_peer(k)
        l2_src[t] = jnp.dot(route(t), points[...], preferred_element_type=F32).astype(BF16)

    part = subs // 8
    cuts = [1, 1 + part, 1 + 3 * part, 1 + 4 * part, 1 + 5 * part, subs]

    def send_part(j):
        @pl.loop(cuts[j], cuts[j + 1])
        def _(k):
            e2(k).start()

    def build_part(lo, hi):
        @pl.loop(lo, hi)
        def _(k):
            build(k)

    build_part(cuts[0], cuts[1])
    send_part(0)

    @pl.loop(1, n)
    def _(k):
        e0(k).wait_recv()

    tile = LANES
    total = n * slots
    per = tile // slots
    k1_dev = cent1.shape[0]

    def targets(lo, count):
        tiles = asked[pl.ds(lo, count)]
        pair = jnp.concatenate([tiles[:, :, c : c + 1] for c in range(CAP)], axis=1)
        return pair.reshape(count * slots, 1)

    @pl.loop(0, total // tile)
    def _(i):
        hot = jnp.where(
            targets(i * per, per) == iota((tile, k1_dev), 1), F32(1), F32(0)
        ).astype(BF16)
        rows = jnp.dot(hot, cent1[...], preferred_element_type=F32).astype(BF16)
        served[pl.ds(i * per, per)] = rows.reshape(per, slots, feat)

    @pl.loop(1, n)
    def _(k):
        e1(k).start()

    fetched[me] = served[me]
    build_part(cuts[1], cuts[2])
    send_part(1)
    build_part(cuts[2], subs)
    build(0)
    l2_dst[s_me] = l2_src[s_me]

    @pl.loop(1, n)
    def _(k):
        e1(k).wait_recv()

    @pl.loop(0, pts // tile)
    def _(i):
        at = pl.ds(pl.multiple_of(i * tile, tile), tile)
        hot = jnp.where(pidx_col[at, :] == iota((tile, total), 1), F32(1), F32(0)).astype(BF16)
        near = jnp.dot(hot, fetched[...].reshape(total, feat), preferred_element_type=F32)
        diff = points[at, :].astype(F32) - near
        spread = jnp.sum(diff * diff, axis=1, keepdims=True) / feat
        w = (1.0 / (1.0 + spread)).astype(BF16).astype(F32)
        eye = iota((tile, tile), 0) == iota((tile, tile), 1)
        w_row[:, at] = jnp.sum(jnp.where(eye, w, F32(0)), axis=0, keepdims=True)

    k3 = groups * rows_a
    tile3 = min(tile, rows_a)
    for j in range(k3 // tile3):
        hot = jnp.where(l3_row[...] == iota((tile3, pts), 0) + j * tile3, w_row[...], F32(0))
        m = jnp.sum(hot, axis=1, keepdims=True)
        s = jnp.dot(hot.astype(BF16), points[...], preferred_element_type=F32)
        g, r = (j * tile3) // rows_a, (j * tile3) % rows_a
        a_src[g, r : r + tile3, :feat] = s.astype(BF16)
        a_src[g, r : r + tile3, feat:] = jnp.broadcast_to(m, (tile3, LANES)).astype(BF16)
    for k in range(1, groups):
        ea(k).start()

    meta_rows = jnp.where(iota((8, pts), 0) == 0, w_row[...], lrows[...]).astype(BF16)

    def meta(k):
        t = sub_peer(k)
        meta_src[t] = lax.dot_general(
            meta_rows, route(t), (((1,), (1,)), ((), ())), preferred_element_type=F32
        )

    @pl.loop(0, total // tile)
    def _(i):
        hot = jnp.where(pidx_row[...] == iota((tile, pts), 0) + i * tile, w_row[...], F32(0))
        m = jnp.sum(hot, axis=1, keepdims=True)
        s = jnp.dot(hot.astype(BF16), points[...], preferred_element_type=F32)
        at = pl.ds(i * per, per)
        back_src[at, :, :feat] = s.astype(BF16).reshape(per, slots, feat)
        back_src[at, :, feat:] = (
            jnp.broadcast_to(m, (tile, LANES)).astype(BF16).reshape(per, slots, LANES)
        )

    for k in range(1, groups):
        ea(k).wait_recv()
    a_dst[g_me] = a_src[g_me]
    acc = a_dst[0].astype(F32)
    for j in range(1, groups):
        acc = acc + a_dst[j].astype(F32)
    for j in range(subs):
        b_src[j] = acc[j * rows_b : (j + 1) * rows_b, :]
    for k in range(1, subs):
        eb(k).start()

    @pl.loop(1, n)
    def _(k):
        e3(k).start()

    back_dst[me] = back_src[me]
    send_part(2)

    @pl.loop(1, subs)
    def _(k):
        meta(k)
        em(k).start()

    meta(0)
    meta_dst[s_me] = meta_src[s_me]

    for k in range(1, subs):
        eb(k).wait_recv()
    b_dst[s_me] = b_src[s_me]
    acc = b_dst[0]
    for j in range(1, subs):
        acc = acc + b_dst[j]
    c_buf[s_me] = (cent3[g_me, s_me] + acc[:, :feat]) / (1.0 + acc[:, feat : feat + 1])
    for k in range(1, subs):
        ec(k).start()
    send_part(3)
    send_part(4)

    @pl.loop(1, n)
    def _(k):
        e3(k).wait_recv()

    tile1 = min(2 * tile, k1_dev)

    def l1_copy(i):
        at = pl.ds(pl.multiple_of(i * tile1, tile1), tile1)
        return pltpu.make_async_copy(l1_buf.at[at], l1_out.at[at], l1sem.at[i])

    @pl.loop(0, k1_dev // tile1)
    def _(i):
        at = pl.ds(pl.multiple_of(i * tile1, tile1), tile1)
        hot = jnp.where(
            targets(0, n) == iota((total, tile1), 1) + i * tile1, F32(1), F32(0)
        ).astype(BF16)
        got = lax.dot_general(
            hot,
            back_dst[...].reshape(total, back_dst.shape[2]),
            (((0,), (0,)), ((), ())),
            preferred_element_type=F32,
        )
        l1_buf[at, :] = (cent1[at, :].astype(F32) + got[:, :feat]) / (1.0 + got[:, feat : feat + 1])
        l1_copy(i).start()

    for k in range(1, subs):
        ec(k).wait_recv()
    for k in range(1, groups):
        ed(k).start()
    own_l3 = pltpu.make_async_copy(c_buf, l3_out.at[g_me], lsem)
    own_l3.start()

    @pl.loop(1, subs)
    def _(k):
        em(k).wait_recv()

    rows2 = cent2.shape[0]
    tile2 = min(2 * tile, rows2)
    acc2[...] = jnp.zeros_like(acc2)
    mass2[...] = jnp.zeros_like(mass2)

    def gather2(t):
        label = meta_dst[t, 1:2, :] * 64.0 + meta_dst[t, 2:3, :]
        weight = meta_dst[t, 0:1, :]
        rows = l2_dst[t]

        @pl.loop(0, rows2 // tile2)
        def _(i):
            at = pl.ds(pl.multiple_of(i * tile2, tile2), tile2)
            hot = jnp.where(
                label == (iota((tile2, cap), 0) + i * tile2).astype(F32), weight, F32(0)
            )
            mass2[at, :] += jnp.sum(hot, axis=1, keepdims=True)
            acc2[at, :] += jnp.dot(hot.astype(BF16), rows, preferred_element_type=F32)

    gather2(s_me)

    @pl.loop(1, subs)
    def _(k):
        e2(k).wait_recv()
        gather2(lax.rem(s_me - k + subs, subs))

    def l2_copy(i):
        at = pl.ds(pl.multiple_of(i * tile2, tile2), tile2)
        return pltpu.make_async_copy(acc2.at[at], l2_new.at[at], l2sem.at[i])

    @pl.loop(0, rows2 // tile2)
    def _(i):
        at = pl.ds(pl.multiple_of(i * tile2, tile2), tile2)
        acc2[at, :] = (cent2[at, :].astype(F32) + acc2[at, :]) / (1.0 + mass2[at, :])
        l2_copy(i).start()

    own_l3.wait()
    for k in range(1, groups):
        ed(k).wait_recv()

    @pl.loop(0, k1_dev // tile1)
    def _(i):
        l1_copy(i).wait()

    @pl.loop(0, rows2 // tile2)
    def _(i):
        l2_copy(i).wait()

    @pl.loop(1, n)
    def _(k):
        e0(k).wait_send()
        e1(k).wait_send()
        e3(k).wait_send()

    @pl.loop(1, subs)
    def _(k):
        e2(k).wait_send()
        em(k).wait_send()
        eb(k).wait_send()
        ec(k).wait_send()

    for k in range(1, groups):
        ea(k).wait_send()
        ed(k).wait_send()


def ranks(hits):
    return jnp.sum(jnp.cumsum(hits, axis=0) * hits, axis=1) - 1


def shards(points, level1_ids, level2_ids, level3_ids, needed, centroids1, centroids2, centroids3, *, k2):
    groups, subs = lax.axis_size("grp"), lax.axis_size("sub")
    n = groups * subs
    pts, feat = points.shape
    k1_dev = centroids1.shape[0]
    k3 = centroids3.shape[0]
    blocks_dev = k1_dev // BLK
    slots = CAP * BLK
    need = needed.shape[1]
    wide = feat + LANES

    wanted = needed[0]
    owners = wanted // blocks_dev
    same = owners[:, None] == owners[None, :]
    before = jnp.arange(need)[None, :] < jnp.arange(need)[:, None]
    places = jnp.sum((same & before).astype(jnp.int32), axis=1)
    slot_index = owners * CAP + places
    requests = jnp.sum(
        jnp.where(
            slot_index[None, :] == jnp.arange(n * CAP)[:, None], (wanted % blocks_dev)[None, :], 0
        ),
        axis=1,
    ).reshape(n, 1, CAP)
    asked = jnp.pad(
        requests * BLK + jnp.arange(BLK, dtype=jnp.int32)[None, :, None],
        ((0, 0), (0, 0), (0, LANES - CAP)),
    )

    entry = level1_ids // BLK
    point_slots = jnp.sum(
        jnp.where(entry[:, None] == jnp.arange(need)[None, :], slot_index[None, :], 0), axis=1
    )
    row_index = point_slots * BLK + level1_ids % BLK

    shard_rows = k2 // subs
    cap = 2 * pts // subs
    range_of = level2_ids // shard_rows
    hits = (range_of[:, None] == jnp.arange(subs)[None, :]).astype(jnp.int32)
    send_index = range_of * cap + ranks(hits)
    local = level2_ids % shard_rows
    lrows = (
        jnp.zeros((8, pts), F32)
        .at[1].set((local // 64).astype(F32))
        .at[2].set((local % 64).astype(F32))
    )

    rows_a = k3 // groups
    rows_b = rows_a // subs
    cent3 = centroids3.astype(F32).reshape(groups, subs, rows_b, feat)
    vmem = pl.BlockSpec(memory_space=pltpu.VMEM)
    anywhere = pl.BlockSpec(memory_space=pl.ANY)
    dma = pltpu.SemaphoreType.DMA
    l1, l2, l3 = pl.pallas_call(
        functools.partial(step_kernel, groups, subs),
        out_shape=(
            jax.ShapeDtypeStruct((k1_dev, feat), F32),
            jax.ShapeDtypeStruct((shard_rows, feat), F32),
            jax.ShapeDtypeStruct((groups, subs, rows_b, feat), F32),
        ),
        in_specs=[vmem] * 10,
        out_specs=[anywhere] * 3,
        scratch_shapes=[
            pltpu.VMEM((n, BLK, LANES), jnp.int32),
            pltpu.VMEM((n, slots, feat), BF16),
            pltpu.VMEM((n, slots, feat), BF16),
            pltpu.VMEM((n, slots, wide), BF16),
            pltpu.VMEM((n, slots, wide), BF16),
            pltpu.VMEM((k1_dev, feat), F32),
            pltpu.VMEM((subs, cap, feat), BF16),
            pltpu.VMEM((subs, cap, feat), BF16),
            pltpu.VMEM((shard_rows, feat), F32),
            pltpu.VMEM((shard_rows, 1), F32),
            pltpu.VMEM((subs, 8, cap), F32),
            pltpu.VMEM((subs, 8, cap), F32),
            pltpu.VMEM((1, pts), F32),
            pltpu.VMEM((groups, rows_a, wide), BF16),
            pltpu.VMEM((groups, rows_a, wide), BF16),
            pltpu.VMEM((subs, rows_b, wide), F32),
            pltpu.VMEM((subs, rows_b, wide), F32),
            pltpu.VMEM((subs, rows_b, feat), F32),
            dma((n,)), dma((n,)), dma((n,)), dma((n,)), dma((n,)), dma((n,)),
            dma((subs,)), dma((subs,)), dma((subs,)), dma((subs,)),
            dma((groups,)), dma((groups,)),
            dma((subs,)), dma((subs,)), dma((subs,)), dma((subs,)),
            dma((groups,)), dma((groups,)),
            dma((k1_dev // 256,)), dma((shard_rows // 256,)), dma,
        ],
        compiler_params=pltpu.CompilerParams(
            collective_id=0, has_side_effects=True, vmem_limit_bytes=60 * 1024 * 1024
        ),
        name="step",
    )(
        asked,
        points,
        row_index[:, None],
        row_index[None, :],
        send_index[None, :],
        level3_ids[None, :],
        lrows,
        centroids1,
        centroids2[0],
        cent3,
    )
    return l1, l2[None], l3.reshape(k3, feat)


def solution(mesh):
    placed = (
        P(("grp", "sub"), None),
        P(("grp", "sub")),
        P(("grp", "sub")),
        P(("grp", "sub")),
        P(("grp", "sub"), None),
        P(("grp", "sub"), None),
        P("grp", "sub", None),
        P(),
    )

    def run(*args):
        return jax.shard_map(
            functools.partial(shards, k2=args[6].shape[1]),
            mesh=mesh,
            in_specs=placed,
            out_specs=(P(("grp", "sub"), None), P("grp", "sub", None), P()),
            check_vma=False,
        )(*args)

    return run
```

```python
import functools

import jax
import jax.numpy as jnp
from jax import lax
from jax.experimental import pallas as pl
from jax.experimental.pallas import tpu as pltpu
from jax.sharding import PartitionSpec as P

BLK = 8
CAP = 2
LANES = 128
MESH = pl.DeviceIdType.MESH
F32 = jnp.float32
BF16 = jnp.bfloat16


def iota(shape, dim):
    return lax.broadcasted_iota(jnp.int32, shape, dim)


def step_kernel(
    groups, subs,
    asked_src, points, pidx_col, pidx_row, sidx_row, l3_row, lrows, cent1, cent2, cent3,
    l1_out, l2_new, l3_out,
    asked, served, fetched, back_src, back_dst, l1_buf,
    l2_src, l2_dst, acc2, mass2, meta_src, meta_dst, w_row,
    a_src, a_dst, b_src, b_dst, c_buf,
    e0s, e0r, e1s, e1r, e3s, e3r, l2s, l2r, ms, mr,
    as_, ar, bs, br, cs, cr, ds_, dr, l1sem, l2sem, lsem,
):
    n = groups * subs
    g_me, s_me = lax.axis_index("grp"), lax.axis_index("sub")
    me = g_me * subs + s_me
    slots = CAP * BLK
    pts, feat = points.shape
    cap = l2_src.shape[1]
    rows_a = a_src.shape[1]
    rows_b = b_src.shape[1]

    def flat(k):
        t = lax.rem(me + k, n)
        return (lax.div(t, subs), lax.rem(t, subs))

    half = subs // 2

    def side(k):
        local = lax.div(k, half + 1)
        base = lax.rem(lax.div(s_me, half) + 1 - local, 2) * half
        return base, k - 1 - local * (half - 1)

    def sub_peer(k):
        base, j = side(k)
        return base + lax.rem(lax.rem(s_me, half) + j, half)

    def sub_source(k):
        base, j = side(k)
        return base + lax.rem(lax.rem(s_me, half) + half - j, half)

    def grp_peer(k):
        return lax.rem(g_me + k, groups)

    barrier = pltpu.get_barrier_semaphore()

    @pl.loop(1, n)
    def _(k):
        pl.semaphore_signal(barrier, inc=1, device_id=flat(k), device_id_type=MESH)

    pl.semaphore_wait(barrier, n - 1)

    def remote(src, dst, ss, rs, dev):
        return pltpu.make_async_remote_copy(
            src_ref=src, dst_ref=dst, send_sem=ss, recv_sem=rs, device_id=dev, device_id_type=MESH
        )

    def e0(k):
        t = lax.rem(me + k, n)
        return remote(asked_src.at[t], asked.at[me], e0s.at[k], e0r.at[k], flat(k))

    def e1(k):
        t = lax.rem(me + k, n)
        return remote(served.at[t], fetched.at[me], e1s.at[k], e1r.at[k], flat(k))

    def e3(k):
        t = lax.rem(me + k, n)
        return remote(back_src.at[t], back_dst.at[me], e3s.at[k], e3r.at[k], flat(k))

    def e2(k):
        t = sub_peer(k)
        return remote(l2_src.at[t], l2_dst.at[s_me], l2s.at[k], l2r.at[k], (g_me, t))

    def em(k):
        t = sub_peer(k)
        return remote(meta_src.at[t], meta_dst.at[s_me], ms.at[k], mr.at[k], (g_me, t))

    def ea(k):
        t = grp_peer(k)
        return remote(a_src.at[t], a_dst.at[g_me], as_.at[k], ar.at[k], (t, s_me))

    def eb(k):
        t = sub_peer(k)
        return remote(b_src.at[t], b_dst.at[s_me], bs.at[k], br.at[k], (g_me, t))

    def ec(k):
        t = sub_peer(k)
        return remote(c_buf.at[s_me], c_buf.at[s_me], cs.at[k], cr.at[k], (g_me, t))

    def ed(k):
        t = grp_peer(k)
        return remote(c_buf, l3_out.at[g_me], ds_.at[k], dr.at[k], (t, s_me))

    @pl.loop(1, n)
    def _(k):
        e0(k).start()

    asked[me] = asked_src[me]

    def route(t):
        slot = iota((cap, pts), 0) + t * cap
        return jnp.where(sidx_row[...] == slot, F32(1), F32(0)).astype(BF16)

    def build(t):
        l2_src[t] = jnp.dot(route(t), points[...], preferred_element_type=F32).astype(BF16)

    part = subs // 8
    parts = [
        (1, 1 + part),
        (1 + part, 1 + 2 * part),
        (half + 1, subs),
        (1 + 2 * part, half + 1),
    ]

    def send_part(j):
        @pl.loop(*parts[j])
        def _(k):
            e2(k).start()

    def build_part(lo, hi):
        @pl.loop(lo, hi)
        def _(k):
            build(sub_peer(k))

    build_part(*parts[0])
    send_part(0)

    @pl.loop(1, n)
    def _(k):
        e0(k).wait_recv()

    tile = LANES
    total = n * slots
    per = tile // slots
    k1_dev = cent1.shape[0]

    def targets(lo, count):
        tiles = asked[pl.ds(lo, count)]
        pair = jnp.concatenate([tiles[:, :, c : c + 1] for c in range(CAP)], axis=1)
        return pair.reshape(count * slots, 1)

    @pl.loop(0, total // tile)
    def _(i):
        hot = jnp.where(
            targets(i * per, per) == iota((tile, k1_dev), 1), F32(1), F32(0)
        ).astype(BF16)
        rows = jnp.dot(hot, cent1[...], preferred_element_type=F32).astype(BF16)
        served[pl.ds(i * per, per)] = rows.reshape(per, slots, feat)

    @pl.loop(1, n)
    def _(k):
        e1(k).start()

    fetched[me] = served[me]
    build_part(*parts[1])
    send_part(1)
    build_part(1 + 2 * part, subs)
    build(s_me)
    l2_dst[s_me] = l2_src[s_me]

    @pl.loop(1, n)
    def _(k):
        e1(k).wait_recv()

    @pl.loop(0, pts // tile)
    def _(i):
        at = pl.ds(pl.multiple_of(i * tile, tile), tile)
        hot = jnp.where(pidx_col[at, :] == iota((tile, total), 1), F32(1), F32(0)).astype(BF16)
        near = jnp.dot(hot, fetched[...].reshape(total, feat), preferred_element_type=F32)
        diff = points[at, :].astype(F32) - near
        spread = jnp.sum(diff * diff, axis=1, keepdims=True) / feat
        w = (1.0 / (1.0 + spread)).astype(BF16).astype(F32)
        eye = iota((tile, tile), 0) == iota((tile, tile), 1)
        w_row[:, at] = jnp.sum(jnp.where(eye, w, F32(0)), axis=0, keepdims=True)

    k3 = groups * rows_a
    tile3 = min(tile, rows_a)
    for j in range(k3 // tile3):
        hot = jnp.where(l3_row[...] == iota((tile3, pts), 0) + j * tile3, w_row[...], F32(0))
        m = jnp.sum(hot, axis=1, keepdims=True)
        s = jnp.dot(hot.astype(BF16), points[...], preferred_element_type=F32)
        g, r = (j * tile3) // rows_a, (j * tile3) % rows_a
        a_src[g, r : r + tile3, :feat] = s.astype(BF16)
        a_src[g, r : r + tile3, feat:] = jnp.broadcast_to(m, (tile3, LANES)).astype(BF16)
    for k in range(1, groups):
        ea(k).start()

    meta_rows = jnp.where(iota((8, pts), 0) == 0, w_row[...], lrows[...]).astype(BF16)

    def meta(t):
        meta_src[t] = lax.dot_general(
            meta_rows, route(t), (((1,), (1,)), ((), ())), preferred_element_type=F32
        )

    @pl.loop(0, total // tile)
    def _(i):
        hot = jnp.where(pidx_row[...] == iota((tile, pts), 0) + i * tile, w_row[...], F32(0))
        m = jnp.sum(hot, axis=1, keepdims=True)
        s = jnp.dot(hot.astype(BF16), points[...], preferred_element_type=F32)
        at = pl.ds(i * per, per)
        back_src[at, :, :feat] = s.astype(BF16).reshape(per, slots, feat)
        back_src[at, :, feat:] = (
            jnp.broadcast_to(m, (tile, LANES)).astype(BF16).reshape(per, slots, LANES)
        )

    for k in range(1, groups):
        ea(k).wait_recv()
    a_dst[g_me] = a_src[g_me]
    acc = a_dst[0].astype(F32)
    for j in range(1, groups):
        acc = acc + a_dst[j].astype(F32)
    for j in range(subs):
        b_src[j] = acc[j * rows_b : (j + 1) * rows_b, :].astype(BF16)
    for k in range(1, subs):
        eb(k).start()

    @pl.loop(1, n)
    def _(k):
        e3(k).start()

    back_dst[me] = back_src[me]
    send_part(2)

    @pl.loop(1, subs)
    def _(k):
        meta(sub_peer(k))
        em(k).start()

    meta(s_me)
    meta_dst[s_me] = meta_src[s_me]

    for k in range(1, subs):
        eb(k).wait_recv()
    b_dst[s_me] = b_src[s_me]
    acc = b_dst[0].astype(F32)
    for j in range(1, subs):
        acc = acc + b_dst[j].astype(F32)
    c_buf[s_me] = (cent3[g_me, s_me] + acc[:, :feat]) / (1.0 + acc[:, feat : feat + 1])
    for k in range(1, subs):
        ec(k).start()
    send_part(3)

    @pl.loop(1, n)
    def _(k):
        e3(k).wait_recv()

    tile1 = min(2 * tile, k1_dev)

    def l1_copy(i):
        at = pl.ds(pl.multiple_of(i * tile1, tile1), tile1)
        return pltpu.make_async_copy(l1_buf.at[at], l1_out.at[at], l1sem.at[i])

    @pl.loop(0, k1_dev // tile1)
    def _(i):
        at = pl.ds(pl.multiple_of(i * tile1, tile1), tile1)
        hot = jnp.where(
            targets(0, n) == iota((total, tile1), 1) + i * tile1, F32(1), F32(0)
        ).astype(BF16)
        got = lax.dot_general(
            hot,
            back_dst[...].reshape(total, back_dst.shape[2]),
            (((0,), (0,)), ((), ())),
            preferred_element_type=F32,
        )
        new = (cent1[at, :].astype(F32) + got[:, :feat]) / (1.0 + got[:, feat : feat + 1])
        l1_buf[at, :] = new.astype(BF16)
        l1_copy(i).start()

    for k in range(1, subs):
        ec(k).wait_recv()
    for k in range(1, groups):
        ed(k).start()
    own_l3 = pltpu.make_async_copy(c_buf, l3_out.at[g_me], lsem)
    own_l3.start()

    @pl.loop(1, subs)
    def _(k):
        em(k).wait_recv()

    rows2 = cent2.shape[0]
    tile2 = min(2 * tile, rows2)
    acc2[...] = jnp.zeros_like(acc2)
    mass2[...] = jnp.zeros_like(mass2)

    def gather2(t):
        label = meta_dst[t, 1:2, :] * 64.0 + meta_dst[t, 2:3, :]
        weight = meta_dst[t, 0:1, :]
        rows = l2_dst[t]

        @pl.loop(0, rows2 // tile2)
        def _(i):
            at = pl.ds(pl.multiple_of(i * tile2, tile2), tile2)
            hot = jnp.where(
                label == (iota((tile2, cap), 0) + i * tile2).astype(F32), weight, F32(0)
            )
            mass2[at, :] += jnp.sum(hot, axis=1, keepdims=True)
            acc2[at, :] += jnp.dot(hot.astype(BF16), rows, preferred_element_type=F32)

    gather2(s_me)

    for span in parts:

        @pl.loop(*span)
        def _(k):
            e2(k).wait_recv()
            gather2(sub_source(k))

    def l2_copy(i):
        at = pl.ds(pl.multiple_of(i * tile2, tile2), tile2)
        return pltpu.make_async_copy(acc2.at[at], l2_new.at[at], l2sem.at[i])

    @pl.loop(0, rows2 // tile2)
    def _(i):
        at = pl.ds(pl.multiple_of(i * tile2, tile2), tile2)
        acc2[at, :] = (cent2[at, :].astype(F32) + acc2[at, :]) / (1.0 + mass2[at, :])
        l2_copy(i).start()

    own_l3.wait()
    for k in range(1, groups):
        ed(k).wait_recv()

    @pl.loop(0, k1_dev // tile1)
    def _(i):
        l1_copy(i).wait()

    @pl.loop(0, rows2 // tile2)
    def _(i):
        l2_copy(i).wait()

    @pl.loop(1, n)
    def _(k):
        e0(k).wait_send()
        e1(k).wait_send()
        e3(k).wait_send()

    @pl.loop(1, subs)
    def _(k):
        e2(k).wait_send()
        em(k).wait_send()
        eb(k).wait_send()
        ec(k).wait_send()

    for k in range(1, groups):
        ea(k).wait_send()
        ed(k).wait_send()


def ranks(hits):
    return jnp.sum(jnp.cumsum(hits, axis=0) * hits, axis=1) - 1


def shards(points, level1_ids, level2_ids, level3_ids, needed, centroids1, centroids2, centroids3, *, k2):
    groups, subs = lax.axis_size("grp"), lax.axis_size("sub")
    n = groups * subs
    pts, feat = points.shape
    k1_dev = centroids1.shape[0]
    k3 = centroids3.shape[0]
    blocks_dev = k1_dev // BLK
    slots = CAP * BLK
    need = needed.shape[1]
    wide = feat + LANES

    wanted = needed[0]
    owners = wanted // blocks_dev
    same = owners[:, None] == owners[None, :]
    before = jnp.arange(need)[None, :] < jnp.arange(need)[:, None]
    places = jnp.sum((same & before).astype(jnp.int32), axis=1)
    slot_index = owners * CAP + places
    requests = jnp.sum(
        jnp.where(
            slot_index[None, :] == jnp.arange(n * CAP)[:, None], (wanted % blocks_dev)[None, :], 0
        ),
        axis=1,
    ).reshape(n, 1, CAP)
    asked = jnp.pad(
        requests * BLK + jnp.arange(BLK, dtype=jnp.int32)[None, :, None],
        ((0, 0), (0, 0), (0, LANES - CAP)),
    )

    entry = level1_ids // BLK
    point_slots = jnp.sum(
        jnp.where(entry[:, None] == jnp.arange(need)[None, :], slot_index[None, :], 0), axis=1
    )
    row_index = point_slots * BLK + level1_ids % BLK

    shard_rows = k2 // subs
    cap = 2 * pts // subs
    range_of = level2_ids // shard_rows
    hits = (range_of[:, None] == jnp.arange(subs)[None, :]).astype(jnp.int32)
    send_index = range_of * cap + ranks(hits)
    local = level2_ids % shard_rows
    lrows = (
        jnp.zeros((8, pts), F32)
        .at[1].set((local // 64).astype(F32))
        .at[2].set((local % 64).astype(F32))
    )

    rows_a = k3 // groups
    rows_b = rows_a // subs
    cent3 = centroids3.astype(F32).reshape(groups, subs, rows_b, feat)
    vmem = pl.BlockSpec(memory_space=pltpu.VMEM)
    anywhere = pl.BlockSpec(memory_space=pl.ANY)
    dma = pltpu.SemaphoreType.DMA
    l1, l2, l3 = pl.pallas_call(
        functools.partial(step_kernel, groups, subs),
        out_shape=(
            jax.ShapeDtypeStruct((k1_dev, feat), BF16),
            jax.ShapeDtypeStruct((shard_rows, feat), F32),
            jax.ShapeDtypeStruct((groups, subs, rows_b, feat), F32),
        ),
        in_specs=[vmem] * 10,
        out_specs=[anywhere] * 3,
        scratch_shapes=[
            pltpu.VMEM((n, BLK, LANES), jnp.int32),
            pltpu.VMEM((n, slots, feat), BF16),
            pltpu.VMEM((n, slots, feat), BF16),
            pltpu.VMEM((n, slots, wide), BF16),
            pltpu.VMEM((n, slots, wide), BF16),
            pltpu.VMEM((k1_dev, feat), BF16),
            pltpu.VMEM((subs, cap, feat), BF16),
            pltpu.VMEM((subs, cap, feat), BF16),
            pltpu.VMEM((shard_rows, feat), F32),
            pltpu.VMEM((shard_rows, 1), F32),
            pltpu.VMEM((subs, 8, cap), F32),
            pltpu.VMEM((subs, 8, cap), F32),
            pltpu.VMEM((1, pts), F32),
            pltpu.VMEM((groups, rows_a, wide), BF16),
            pltpu.VMEM((groups, rows_a, wide), BF16),
            pltpu.VMEM((subs, rows_b, wide), BF16),
            pltpu.VMEM((subs, rows_b, wide), BF16),
            pltpu.VMEM((subs, rows_b, feat), F32),
            dma((n,)), dma((n,)), dma((n,)), dma((n,)), dma((n,)), dma((n,)),
            dma((subs,)), dma((subs,)), dma((subs,)), dma((subs,)),
            dma((groups,)), dma((groups,)),
            dma((subs,)), dma((subs,)), dma((subs,)), dma((subs,)),
            dma((groups,)), dma((groups,)),
            dma((k1_dev // 256,)), dma((shard_rows // 256,)), dma,
        ],
        compiler_params=pltpu.CompilerParams(
            collective_id=0, has_side_effects=True, vmem_limit_bytes=60 * 1024 * 1024
        ),
        name="step",
    )(
        asked,
        points,
        row_index[:, None],
        row_index[None, :],
        send_index[None, :],
        level3_ids[None, :],
        lrows,
        centroids1,
        centroids2[0],
        cent3,
    )
    return l1.astype(F32), l2[None], l3.reshape(k3, feat)


def solution(mesh):
    placed = (
        P(("grp", "sub"), None),
        P(("grp", "sub")),
        P(("grp", "sub")),
        P(("grp", "sub")),
        P(("grp", "sub"), None),
        P(("grp", "sub"), None),
        P("grp", "sub", None),
        P(),
    )

    def run(*args):
        return jax.shard_map(
            functools.partial(shards, k2=args[6].shape[1]),
            mesh=mesh,
            in_specs=placed,
            out_specs=(P(("grp", "sub"), None), P("grp", "sub", None), P()),
            check_vma=False,
        )(*args)

    return run
```
